256 devices in a mesh: outer: 4 (over y_lo, core), inner: 64 (over x, y_hi, z).
Axes of the slice: x: 4, y: 4 (y_hi: 2, y_lo: 2; y = y_hi * 2 + y_lo), z: 8, core: 2. Of those that a mesh axis runs over, the one named last changes fastest.
Arguments:
- layer_input: bfloat16 [8192, 256, 192], P(('outer', 'inner')), may hold values from -6 to 6
- out_grad: bfloat16 [8192, 256, 192], P(('outer', 'inner')), may hold values from -6 to 6
- mix_weight: bfloat16 [256, 128], replicated, may hold values from -0.375 to 0.375
- lift_weight: bfloat16 [128, 192], replicated, may hold values from -0.5 to 0.5
- linear_weight: bfloat16 [256, 256], replicated, may hold values from -0.375 to 0.375
- row_ids: int32 [8192, 256], P(('outer', 'inner')), may hold values from 0 to 131071, as said below
- row_home: int32 [131072], replicated, may hold values from 0 to 131071, as said below
- table: float32 [131072, 192], P('inner'), may hold values from -0.6 to 0.6
- row_accum: float32 [131072], P('inner'), may hold values from 1 to 100
Outputs:
- new_table: float32 [131072, 192], P('inner')
- new_accum: float32 [131072], P('inner')
- mix_grad: float32 [256, 128], replicated
- lift_grad: float32 [128, 192], replicated
- linear_grad: float32 [256, 256], replicated
The draws below stay inside these ranges and needn't reach their ends.
Inputs may be any that keep to these rules, and one draw needn't show every extreme that they name: row_home is a permutation: hashed row i is stored at position row_home[i], held by inner index row_home[i] // 2048. In each aligned block of 16 samples (all their features together), every inner index is the owner, row_home[row_ids] // 2048, of exactly 64 lookups. The same row may be named many times.
All inputs are finite; a program needn't handle non-finite values.
Results may differ from the reference program's by a relative error of at most 0.0041.
Values may be sent and summed in bfloat16 or wider, within the bound.
A program may use at most 64 MiB of HBM per device.

```python
import math
import jax
import jax.numpy as jnp
from jax import lax

FEATS = 256
D = 192
RANK = 128
SAMP_DEV = 32
ROWS_DEV = 2048
BATCH = 8192
ROWS = 131072
N_INNER = 64


def shared_rows(key):
    base = jax.random.fold_in(key, 911)
    k_perm, k_owner, k_first, k_second, k_third = jax.random.split(base, 5)
    row_home = jax.random.permutation(k_perm, ROWS).astype(jnp.int32)
    inverse = jnp.zeros((ROWS,), jnp.int32).at[row_home].set(jnp.arange(ROWS, dtype=jnp.int32))
    per_half = SAMP_DEV // 2 * FEATS
    blocks = BATCH // (SAMP_DEV // 2)
    pattern = jnp.arange(per_half, dtype=jnp.int32) % N_INNER
    owner_keys = jax.random.split(k_owner, blocks)
    owners = jax.vmap(lambda sub_key: jax.random.permutation(sub_key, pattern))(owner_keys)
    shape_all = (blocks, per_half)
    local_rows = jnp.minimum(jax.random.randint(k_first, shape_all, 0, ROWS_DEV), jax.random.randint(k_second, shape_all, 0, ROWS_DEV))
    local_rows = jnp.minimum(local_rows, jax.random.randint(k_third, shape_all, 0, ROWS_DEV))
    places = (owners * ROWS_DEV + local_rows).astype(jnp.int32)
    row_ids = jnp.take(inverse, places.reshape(-1), axis=0).reshape(BATCH, FEATS)
    return (row_ids.astype(jnp.int32), row_home)


def draw_row_ids(key, part):
    return shared_rows(key)[0]


def draw_row_home(key, part):
    return shared_rows(key)[1]


def levels(key, dims, cuts, least, top_value):
    factor_of, own = 1.0, jax.random.fold_in(key, 6)
    for axis_at, parts in cuts:
        draws = jnp.exp(jax.random.uniform(jax.random.fold_in(own, axis_at), (parts,), jnp.float32, least / len(cuts), top_value / len(cuts)))
        factor_of = factor_of * jnp.repeat(draws, dims[axis_at] // parts).reshape([-1 if axis == axis_at else 1 for axis in range(len(dims))])
    return factor_of


def bell_draw(own_key, dims, scale, reach, cuts=(), kind=jnp.bfloat16):
    entries = scale * jax.random.normal(own_key, dims, jnp.float32)
    if cuts:
        entries = entries * levels(own_key, dims, cuts, -0.22, 0.18)
    return jnp.clip(entries, -reach, reach).astype(kind)


def setup_inputs(seed: int = 0) -> dict:
    splits = jax.random.split(jax.random.key(seed), 10)
    layer_input = bell_draw(splits[0], (BATCH, FEATS, D), 1.0, 6.0, ((0, 256),))
    out_grad = bell_draw(splits[1], (BATCH, FEATS, D), 1.0, 6.0, ((0, 256),))
    mix_weight = bell_draw(splits[2], (FEATS, RANK), FEATS ** -0.5, 0.375)
    lift_weight = bell_draw(splits[3], (RANK, D), RANK ** -0.5, 0.5)
    linear_weight = bell_draw(splits[4], (FEATS, FEATS), FEATS ** -0.5, 0.375)
    row_ids = draw_row_ids(jax.random.fold_in(splits[9], 71), 0)
    row_home = draw_row_home(jax.random.fold_in(splits[9], 71), 0)
    table = bell_draw(splits[7], (ROWS, D), 0.1, 0.6, ((0, 64),), jnp.float32)
    row_accum = jnp.clip(jnp.exp(math.log(100.0) - 4.6051702 * jax.random.uniform(splits[8], (ROWS,), jnp.float32) ** levels(splits[8], (ROWS,), ((0, 64),), -0.2, 0.2)), 1.0, 100.0)
    return {"layer_input": layer_input, "out_grad": out_grad, "mix_weight": mix_weight, "lift_weight": lift_weight, "linear_weight": linear_weight, "row_ids": row_ids, "row_home": row_home, "table": table, "row_accum": row_accum}


LEARN_RATE = 0.5

def to_half(values):
    return lax.optimization_barrier(values.astype(jnp.bfloat16)).astype(jnp.float32)

def reference(layer_input, out_grad, mix_weight, lift_weight, linear_weight, row_ids, row_home, table, row_accum):
    scaling = 1.0 / math.sqrt(D)
    blocks = BATCH // SAMP_DEV
    inputs_all = layer_input.reshape(blocks, SAMP_DEV, FEATS, D)
    grads_all = out_grad.reshape(blocks, SAMP_DEV, FEATS, D)
    places_all = jnp.take(row_home, row_ids.reshape(-1), axis=0).astype(jnp.int32).reshape(blocks, SAMP_DEV * FEATS)
    mixing = mix_weight.astype(jnp.float32)
    lifting = lift_weight.astype(jnp.float32)
    linear = linear_weight.astype(jnp.float32)

    def step(carry, item):
        g_mix, g_lift, g_linear, g_table = carry
        inputs_blk, grads_blk, places = item
        inputs = inputs_blk.astype(jnp.float32)
        cotangent = grads_blk.astype(jnp.float32)
        compressed = to_half(jnp.einsum('bfd,fk->bdk', inputs, mixing))
        products = to_half(jnp.einsum('bfd,bdk->bfk', inputs, compressed) * scaling)
        d_products = to_half(jnp.einsum('bfd,kd->bfk', cotangent, lifting))
        d_compressed = to_half(jnp.einsum('bfd,bfk->bdk', inputs, d_products) * scaling)
        d_inputs = cotangent + jnp.einsum('fg,bfd->bgd', linear, cotangent)
        d_inputs = d_inputs + scaling * jnp.einsum('bfk,bdk->bfd', d_products, compressed)
        d_inputs = d_inputs + jnp.einsum('fk,bdk->bfd', mixing, d_compressed)
        g_mix = g_mix + jnp.einsum('bfd,bdk->fk', inputs, d_compressed)
        g_lift = g_lift + jnp.einsum('bfk,bfd->kd', products, cotangent)
        g_linear = g_linear + jnp.einsum('bfd,bgd->fg', cotangent, inputs)
        rounded = to_half(d_inputs).reshape(-1, D)
        g_table = g_table.at[places].add(rounded)
        return ((g_mix, g_lift, g_linear, g_table), None)
    start = (jnp.zeros((FEATS, RANK), jnp.float32), jnp.zeros((RANK, D), jnp.float32), jnp.zeros((FEATS, FEATS), jnp.float32), jnp.zeros((ROWS, D), jnp.float32))
    (g_mix, g_lift, g_linear, g_table), unused = lax.scan(step, start, (inputs_all, grads_all, places_all))
    new_accum = row_accum + lax.optimization_barrier(jnp.mean(g_table * g_table, axis=1))
    new_table = table - LEARN_RATE * g_table / jnp.sqrt(new_accum)[:, None]
    return (new_table, new_accum, g_mix / BATCH, g_lift / BATCH, g_linear / BATCH)
```

```python
import math

import jax
import jax.numpy as jnp
from jax import lax
from jax.experimental import pallas as pl
from jax.experimental.pallas import tpu as pltpu
from jax.sharding import PartitionSpec as P

LEARN_RATE = 0.5
MESH = pl.DeviceIdType.MESH
BF = jnp.bfloat16
F32 = jnp.float32
VM = pl.BlockSpec(memory_space=pltpu.VMEM)

SAMPLES, FEATS, WIDTH, RANK = 32, 256, 192, 128
BATCH = 8192
HALF = 4096
PACK = 1536
PIECE = 768


def dot(a, b, dims=((1,), (0,))):
    return lax.dot_general(a, b, (dims, ((), ())), preferred_element_type=F32)


NT = ((1,), (1,))


def iota(shape, axis):
    return lax.broadcasted_iota(jnp.int32, shape, axis)


def index_kernel(ids_ref, home_ref, key_ref, local_ref, table_t, place_ref):
    home = home_ref[...]
    high = (home >> 9).astype(F32)
    low = ((home & 511) - 256).astype(F32)
    table_t[0:128, :] = high.T.astype(BF)
    table_t[128:256, :] = low.T.astype(BF)
    rows1024 = iota((1024, 256), 0)
    rows128 = iota((128, 256), 0)

    def look(b, carry):
        ids = ids_ref[pl.ds(b, 1), :]
        hot = (rows1024 == (ids >> 7)).astype(F32).astype(BF)
        found = dot(table_t[...], hot)
        mask = rows128 == (ids & 127)
        high_part = jnp.sum(jnp.where(mask, found[0:128], 0.0), axis=0, keepdims=True)
        low_part = jnp.sum(jnp.where(mask, found[128:256], 0.0), axis=0, keepdims=True)
        place_ref[pl.ds(b, 1), :] = (high_part * 512.0 + low_part + 256.0).astype(jnp.int32)
        return carry

    lax.fori_loop(0, SAMPLES, look, 0, unroll=4)
    upper = (iota((256, 256), 0) < iota((256, 256), 1)).astype(F32).astype(BF)
    rows64 = iota((64, 256), 0)
    for half in range(2):

        def rank(step, carry):
            counts, firsts = carry
            b = half * 16 + step
            place = place_ref[pl.ds(b, 1), :]
            owner = place >> 11
            local = place & 2047
            own = (rows64 == owner).astype(F32)
            before = dot(own.astype(BF), upper) + counts
            rank_of = jnp.sum(own * before, axis=0, keepdims=True).astype(jnp.int32)
            key_ref[pl.ds(b, 1), :] = (owner & 7) * 512 + (owner >> 3) * 64 + rank_of
            hot = (rows64 == rank_of).astype(F32).astype(BF)
            parts = jnp.concatenate(
                [own * (local >> 4).astype(F32), own * (local & 15).astype(F32)], axis=0
            ).astype(BF)
            firsts = firsts + dot(parts, hot, NT)
            counts = counts + jnp.sum(own, axis=1, keepdims=True)
            return counts, firsts

        start = (jnp.zeros((64, 1), F32), jnp.zeros((128, 64), F32))
        unused, firsts = lax.fori_loop(0, 16, rank, start, unroll=4)
        merged = firsts[0:64] * 16.0 + firsts[64:128]
        local_ref[:, half * 64 : (half + 1) * 64] = merged.astype(jnp.int32)


def index_call(row_ids, home):
    return pl.pallas_call(
        index_kernel,
        out_shape=(
            jax.ShapeDtypeStruct((SAMPLES, FEATS), jnp.int32),
            jax.ShapeDtypeStruct((64, 128), jnp.int32),
        ),
        in_specs=[VM, VM],
        out_specs=(VM, VM),
        scratch_shapes=[pltpu.VMEM((256, 1024), BF), pltpu.VMEM((SAMPLES, FEATS), jnp.int32)],
        compiler_params=pltpu.CompilerParams(vmem_limit_bytes=32 * 2**20),
        name="index",
    )(row_ids, home)


def layer_kernel(x_ref, g_ref, mix_ref, mix_t_ref, lift_ref, lift_t_ref, linear_t_ref, rows_ref, dense_ref):
    scaling = 1.0 / math.sqrt(WIDTH)

    @pl.when(pl.program_id(0) == 0)
    def _():
        dense_ref[...] = jnp.zeros_like(dense_ref)

    x = x_ref[0]
    g = g_ref[0]
    d_products = dot(g, lift_t_ref[...]).astype(BF)
    d_products_t = dot(lift_ref[...], g, NT).astype(BF)
    both = dot(jnp.concatenate([mix_t_ref[...], d_products_t], axis=0), x)
    compressed_t = both[0:128].astype(BF)
    d_compressed_t = (both[128:256] * scaling).astype(BF)
    products_t = (dot(compressed_t, x, NT) * scaling).astype(BF)
    d_inputs = g.astype(F32) + dot(linear_t_ref[...], g)
    d_inputs = d_inputs + scaling * dot(d_products, compressed_t)
    d_inputs = d_inputs + dot(mix_ref[...], d_compressed_t)
    rows_ref[...] = jnp.concatenate([d_inputs, d_inputs[:, 128:192]], axis=1).astype(BF)
    dense_ref[0:256] += dot(x, d_compressed_t, NT)
    linear = dot(g, x, NT)
    dense_ref[256:512] += linear[:, 0:128]
    dense_ref[512:768] += linear[:, 128:256]
    lift = dot(products_t, g)
    dense_ref[768:896] += lift[:, 0:128]
    dense_ref[896:1024, 0:64] += lift[:, 128:192]


def layer_call(x, g, mix, lift, linear):
    whole = lambda shape: pl.BlockSpec(shape, lambda b: (0, 0))
    return pl.pallas_call(
        layer_kernel,
        grid=(SAMPLES,),
        out_shape=(
            jax.ShapeDtypeStruct((SAMPLES * FEATS, 256), BF),
            jax.ShapeDtypeStruct((1024, 128), F32),
        ),
        in_specs=[
            pl.BlockSpec((1, FEATS, WIDTH), lambda b: (b, 0, 0)),
            pl.BlockSpec((1, FEATS, WIDTH), lambda b: (b, 0, 0)),
            whole((256, 128)),
            whole((128, 256)),
            whole((128, 192)),
            whole((192, 128)),
            whole((256, 256)),
        ],
        out_specs=(pl.BlockSpec((FEATS, 256), lambda b: (b, 0)), whole((1024, 128))),
        compiler_params=pltpu.CompilerParams(
            vmem_limit_bytes=32 * 2**20, dimension_semantics=("arbitrary",)
        ),
        name="layer",
    )(x, g, mix, mix.T, lift, lift.T, linear.T)


class Spot:
    def __init__(self):
        outer = lax.axis_index("outer")
        inner = lax.axis_index("inner")
        self.core = lax.rem(outer, 2)
        self.y_lo = outer // 2
        self.x = inner // 16
        self.y_hi = lax.rem(inner // 8, 2)
        self.z = lax.rem(inner, 8)
        self.y = self.y_hi * 2 + self.y_lo

    def at(self, x=None, y=None, z=None, core=None):
        x = self.x if x is None else x
        y = self.y if y is None else y
        z = self.z if z is None else z
        core = self.core if core is None else core
        return (lax.rem(y, 2) * 2 + core, (x * 2 + y // 2) * 8 + z)


def chunk_offset(i):
    return 4 + (1 - 2 * (i % 2)) * ((i + 1) // 2)


def exchange_kernel(
    key_ref, local_ref, rows_ref, dense_ref, table_ref, accum_ref,
    new_table_ref, new_accum_ref, mix_ref, lift_ref, linear_ref,
    send, recv, local_in, rhs, own, across, across_in, ring_out, ring_in,
    finish, chip_in, core_in, core_in2,
    d_half, d_half_in, d_y_in, d_y, d_x_in, d_z, d_xg, d_yg, d_cg,
    s_send, s_recv, i_send, i_recv, a_send, a_recv, r_send, r_recv, f_send, f_recv, d_send, d_recv,
):
    me = Spot()
    x, y, z, core = me.x, me.y, me.z, me.core
    lanes = iota((256, 128), 1)
    iota_rows = iota((256, 128), 0).astype(F32).astype(BF)

    def peer(k):
        dx, dy = k // 2, k % 2
        y_to = me.y if dy == 0 else (1 - me.y_hi) * 2 + (1 - me.y_lo)
        return me.at(x=lax.rem(x + dx, 4), y=y_to)

    def place_of(k):
        dx, dy = k // 2, k % 2
        return lax.rem(x + dx, 4) * 2 + (me.y_hi if dy == 0 else 1 - me.y_hi)

    partner = me.at(core=1 - core)
    beside = me.at(y=me.y_hi * 2 + 1 - me.y_lo)
    up = me.at(z=lax.rem(z + 1, 8))
    down = me.at(z=lax.rem(z + 7, 8))
    y_peer = lambda k: me.at(y=lax.rem(y + k, 4))
    x_peer = lambda k: me.at(x=lax.rem(x + k, 4))
    z_peer = lambda k: me.at(z=lax.rem(z + k, 8))

    barrier = pltpu.get_barrier_semaphore()
    greeted = (
        [peer(k) for k in range(1, 8)]
        + [partner]
        + [y_peer(k) for k in (1, 2, 3)]
        + [x_peer(k) for k in (1, 2, 3)]
        + [z_peer(k) for k in range(1, 8)]
    )
    for device in greeted:
        pl.semaphore_signal(barrier, inc=1, device_id=device, device_id_type=MESH)
    pl.semaphore_wait(barrier, len(greeted))

    def copy(src, dst, send_sem, recv_sem, device):
        return pltpu.make_async_remote_copy(
            src_ref=src, dst_ref=dst, send_sem=send_sem, recv_sem=recv_sem,
            device_id=device, device_id_type=MESH,
        )

    def index_copy(k):
        return copy(local_ref.at[place_of(k)], local_in.at[k], i_send.at[k], i_recv.at[k], peer(k))

    def lookup_copy(i, k):
        return copy(send.at[i, place_of(k)], recv.at[i, k], s_send.at[i, k], s_recv.at[i, k], peer(k))

    def across_copy(i):
        return copy(across.at[i], across_in.at[i], a_send.at[i], a_recv.at[i], partner)

    def ring_copy(way, slot):
        return copy(
            ring_out.at[way, slot], ring_in.at[way, slot], r_send.at[way, slot], r_recv.at[way, slot],
            (up, down)[way],
        )

    def chip_copy(p):
        return copy(finish.at[p], chip_in.at[p], f_send.at[0, p], f_recv.at[0, p], beside)

    def core_copy(p):
        return copy(finish.at[p], core_in.at[p], f_send.at[1, p], f_recv.at[1, p], partner)

    def forward_copy(p):
        return copy(chip_in.at[p], core_in2.at[p], f_send.at[2, p], f_recv.at[2, p], partner)

    def half_copy():
        return copy(dense_ref.at[1 - core], d_half_in, d_send.at[0], d_recv.at[0], partner)

    def y_copy(k):
        return copy(d_half.at[lax.rem(y + k, 4)], d_y_in.at[k - 1], d_send.at[k], d_recv.at[k], y_peer(k))

    def x_copy(k):
        return copy(d_y.at[lax.rem(x + k, 4)], d_x_in.at[k - 1], d_send.at[3 + k], d_recv.at[3 + k], x_peer(k))

    def z_copy(k):
        return copy(d_z.at[z], d_z.at[z], d_send.at[6 + k], d_recv.at[6 + k], z_peer(k))

    def z_wait(k):
        return copy(d_z.at[z], d_z.at[lax.rem(z + 8 - k, 8)], d_send.at[6 + k], d_recv.at[6 + k], z_peer(k))

    def xg_copy(k):
        return copy(d_xg.at[x], d_xg.at[x], d_send.at[13 + k], d_recv.at[13 + k], x_peer(k))

    def xg_wait(k):
        return copy(d_xg.at[x], d_xg.at[lax.rem(x + 4 - k, 4)], d_send.at[13 + k], d_recv.at[13 + k], x_peer(k))

    def yg_copy(k):
        return copy(d_yg.at[y], d_yg.at[y], d_send.at[16 + k], d_recv.at[16 + k], y_peer(k))

    def yg_wait(k):
        return copy(d_yg.at[y], d_yg.at[lax.rem(y + 4 - k, 4)], d_send.at[16 + k], d_recv.at[16 + k], y_peer(k))

    def cg_copy():
        return copy(d_cg.at[core], d_cg.at[core], d_send.at[20], d_recv.at[20], partner)

    def cg_wait():
        return copy(d_cg.at[core], d_cg.at[1 - core], d_send.at[20], d_recv.at[20], partner)

    def dense_1():
        half_copy().start()

    def dense_2():
        half_copy().wait_recv()
        total = dense_ref[core] + d_half_in[...]
        d_half[...] = total.reshape(4, 128, 128)
        for k in (1, 2, 3):
            y_copy(k).start()

    def dense_3():
        for k in (1, 2, 3):
            y_copy(k).wait_recv()
        total = d_half[y] + d_y_in[0] + d_y_in[1] + d_y_in[2]
        d_y[...] = total.reshape(4, 32, 128)
        for k in (1, 2, 3):
            x_copy(k).start()

    def dense_4():
        for k in (1, 2, 3):
            x_copy(k).wait_recv()
        d_z[z] = d_y[x] + d_x_in[0] + d_x_in[1] + d_x_in[2]
        for k in range(1, 8):
            z_copy(k).start()

    def dense_5():
        for k in range(1, 8):
            z_wait(k).wait_recv()
        total = d_z[0]
        for k in range(1, 8):
            total = total + d_z[k]
        d_xg[x] = total * (1.0 / BATCH)
        for k in (1, 2, 3):
            xg_copy(k).start()

    def dense_6():
        for k in (1, 2, 3):
            xg_wait(k).wait_recv()
        d_yg[y] = d_xg[...].reshape(128, 128)
        for k in (1, 2, 3):
            yg_copy(k).start()

    def dense_7():
        for k in (1, 2, 3):
            yg_wait(k).wait_recv()
        d_cg[core] = d_yg[...].reshape(512, 128)
        cg_copy().start()

    def dense_8():
        cg_wait().wait_recv()
        mix_ref[...] = d_cg[0, 0:256]
        linear_ref[:, 0:128] = d_cg[0, 256:512]
        linear_ref[:, 128:256] = d_cg[1, 0:256]
        lift_ref[:, 0:128] = d_cg[1, 256:384]
        lift_ref[:, 128:192] = d_cg[1, 384:512, 0:64]

    def one_hot(row, base):
        near = (row - base).astype(F32).astype(BF)
        tiles = []
        for t in range(row.shape[1] // 128):
            part = jnp.broadcast_to(near[:, t * 128 : (t + 1) * 128], (256, 128))
            tiles.append(jnp.where(iota_rows == part, jnp.ones((), BF), jnp.zeros((), BF)))
        return jnp.concatenate(tiles, axis=1)

    def sort_chunk(i):
        to = lax.rem(z + chunk_offset(i), 8)
        for part in range(2):
            base = to * 512 + part * 256
            got = []
            for half in range(2):
                total = jnp.zeros((256, 256), F32)
                for t in range(4):
                    hot = jnp.concatenate(
                        [
                            one_hot(key_ref[pl.ds(half * 16 + t * 4 + b, 1), :], base)
                            for b in range(4)
                        ],
                        axis=1,
                    )
                    start = half * HALF + t * 1024
                    total = total + dot(hot, rows_ref[start : start + 1024, :])
                got.append(total)
            tail = jnp.where(lanes < 64, got[0][:, 128:256], got[1][:, 128:256]).astype(BF)
            for q in range(4):
                at = slice(q * 64, (q + 1) * 64)
                send[i, part * 4 + q, 0:64, :] = got[0][at, 0:128].astype(BF)
                send[i, part * 4 + q, 64:128, :] = got[1][at, 0:128].astype(BF)
                send[i, part * 4 + q, 128:192, :] = tail[at]

    def add_chunk(i):
        to = lax.rem(z + chunk_offset(i), 8)
        lane64 = iota((64, 128), 1) < 64
        where = []
        for k in range(8):
            if k == 0:
                block = send.at[i, place_of(0)]
                where.append(local_ref[place_of(0), pl.ds(to, 1), :])
            else:
                lookup_copy(i, k).wait_recv()
                block = recv.at[i, k]
                where.append(local_in[k, pl.ds(to, 1), :])
            rhs[k * 128 : (k + 1) * 128, 0:128] = block[0:128]
            tail = block[128:192].astype(F32)
            turned = pltpu.roll(tail, 64, 1)
            rhs[k * 128 : k * 128 + 64, 128:256] = jnp.where(lane64, tail, turned).astype(BF)
            rhs[k * 128 + 64 : (k + 1) * 128, 128:256] = jnp.where(lane64, turned, tail).astype(BF)
        row = jnp.concatenate(where, axis=1)
        for mine in (False, True):
            first = (core if mine else 1 - core) * 1024
            for m in range(2):
                hot = jnp.concatenate(
                    [one_hot(row, first + m * 256), one_hot(row, first + 512 + m * 256)], axis=0
                )
                total = dot(hot, rhs[...])
                tail = jnp.where(lanes < 64, total[0:256, 128:256], total[256:512, 128:256])
                ends = ((m * 256, total[0:256, 0:128]), (512 + m * 256, total[256:512, 0:128]), (1024 + m * 256, tail))
                for start, value in ends:
                    if mine:
                        own[i, start : start + 256, :] = value
                    else:
                        across[i, start : start + 256, :] = value.astype(BF)

    def pieces(i, p):
        at = slice(p * PIECE, (p + 1) * PIECE)
        return own[i, at, :] + across_in[i, at, :].astype(F32)

    for k in range(1, 8):
        index_copy(k).start()
    dense_1()

    def sort_step(i, carry):
        sort_chunk(i)
        for k in range(1, 8):
            lookup_copy(i, k).start()
        return carry

    lax.fori_loop(0, 2, sort_step, 0)
    dense_2()
    lax.fori_loop(2, 4, sort_step, 0)
    dense_3()
    lax.fori_loop(4, 8, sort_step, 0)
    for k in range(1, 8):
        index_copy(k).wait_recv()

    def add_step(i, carry):
        add_chunk(i)
        across_copy(i).start()
        return carry

    def ring_send(way, slot, value):
        ring_out[way, slot] = value.astype(BF)
        ring_copy(way, slot).start()

    def ring_got(way, slot):
        ring_copy(way, slot).wait_recv()
        return ring_in[way, slot].astype(F32)

    lax.fori_loop(0, 1, add_step, 0)
    across_copy(0).wait_recv()
    ring_send(0, 0, pieces(0, 0))
    ring_send(1, 0, pieces(0, 1))
    for level in range(3):
        lax.fori_loop(1 + 2 * level, 3 + 2 * level, add_step, 0)
        for i in (1 + 2 * level, 2 + 2 * level):
            across_copy(i).wait_recv()
        for slot in (1 + 2 * level, 2 + 2 * level):
            for way in range(2):
                value = pieces(1 + 2 * level + way, (slot + way) % 2)
                if slot >= 2:
                    value = value + ring_got(way, slot - 2)
                ring_send(way, slot, value)
        if level == 0:
            dense_4()
        elif level == 1:
            dense_5()
    lax.fori_loop(7, 8, add_step, 0)
    dense_6()
    across_copy(7).wait_recv()
    for p in (1, 0):
        total = pieces(7, p) + ring_got(0, 6 - p) + ring_got(1, 5 + p)
        finish[p] = total.astype(BF)
        chip_copy(p).start()
        core_copy(p).start()
    dense_7()
    for p in (1, 0):
        chip_copy(p).wait_recv()
        forward_copy(p).start()

    eye = iota((128, 128), 0) == iota((128, 128), 1)
    lane128 = iota((128, 128), 1) < 64

    def update(half, first, second):
        for m in range(8):
            def packed(ref, start):
                return ref[start // PIECE, start % PIECE : start % PIECE + 128, :].astype(F32)

            main = packed(first, m * 128) + packed(second, m * 128)
            at = 1024 + (m % 4) * 128
            tail = packed(first, at) + packed(second, at)
            if m >= 4:
                tail = pltpu.roll(tail, 64, 1)
            square = main * main + jnp.where(lane128, tail * tail, 0.0)
            mean = jnp.sum(square, axis=1, keepdims=True) * (1.0 / WIDTH)
            before = jnp.broadcast_to(accum_ref[pl.ds(half * 8 + m, 1), :], (128, 128))
            before = jnp.sum(jnp.where(eye, before, 0.0), axis=1, keepdims=True)
            after = before + mean
            shown = jnp.broadcast_to(after, (128, 128))
            new_accum_ref[pl.ds(half * 8 + m, 1), :] = jnp.sum(
                jnp.where(eye, shown, 0.0), axis=0, keepdims=True
            )
            rate = LEARN_RATE / jnp.sqrt(after)
            rows = pl.ds(pl.multiple_of(half * 1024 + m * 128, 128), 128)
            new_table_ref[rows, 0:128] = table_ref[rows, 0:128] - main * rate
            new_table_ref[rows, 128:192] = table_ref[rows, 128:192] - (tail * rate)[:, 0:64]

    update(core, finish, chip_in)
    for p in (1, 0):
        core_copy(p).wait_recv()
        forward_copy(p).wait_recv()
    update(1 - core, core_in, core_in2)
    dense_8()

    for k in range(1, 8):
        index_copy(k).wait_send()
        z_copy(k).wait_send()

    def sent(i, carry):
        for k in range(1, 8):
            lookup_copy(i, k).wait_send()
        across_copy(i).wait_send()
        return carry

    lax.fori_loop(0, 8, sent, 0)
    for way in range(2):
        for slot in range(7):
            ring_copy(way, slot).wait_send()
    for p in range(2):
        chip_copy(p).wait_send()
        core_copy(p).wait_send()
        forward_copy(p).wait_send()
    half_copy().wait_send()
    for k in (1, 2, 3):
        y_copy(k).wait_send()
        x_copy(k).wait_send()
        xg_copy(k).wait_send()
        yg_copy(k).wait_send()
    cg_copy().wait_send()


def exchange_call(key, local, rows, dense, table, accum):
    dma = pltpu.SemaphoreType.DMA
    vmem = pltpu.VMEM
    return pl.pallas_call(
        exchange_kernel,
        out_shape=(
            jax.ShapeDtypeStruct((2048, WIDTH), F32),
            jax.ShapeDtypeStruct((16, 128), F32),
            jax.ShapeDtypeStruct((256, 128), F32),
            jax.ShapeDtypeStruct((128, 192), F32),
            jax.ShapeDtypeStruct((256, 256), F32),
        ),
        in_specs=[VM] * 6,
        out_specs=(VM,) * 5,
        scratch_shapes=[
            vmem((8, 8, 192, 128), BF),
            vmem((8, 8, 192, 128), BF),
            vmem((8, 8, 128), jnp.int32),
            vmem((1024, 256), BF),
            vmem((8, PACK, 128), F32),
            vmem((8, PACK, 128), BF),
            vmem((8, PACK, 128), BF),
            vmem((2, 7, PIECE, 128), BF),
            vmem((2, 7, PIECE, 128), BF),
            vmem((2, PIECE, 128), BF),
            vmem((2, PIECE, 128), BF),
            vmem((2, PIECE, 128), BF),
            vmem((2, PIECE, 128), BF),
            vmem((4, 128, 128), F32),
            vmem((512, 128), F32),
            vmem((3, 128, 128), F32),
            vmem((4, 32, 128), F32),
            vmem((3, 32, 128), F32),
            vmem((8, 32, 128), F32),
            vmem((4, 32, 128), F32),
            vmem((4, 128, 128), F32),
            vmem((2, 512, 128), F32),
            dma((8, 8)), dma((8, 8)), dma((8,)), dma((8,)), dma((8,)), dma((8,)),
            dma((2, 7)), dma((2, 7)), dma((3, 2)), dma((3, 2)), dma((21,)), dma((21,)),
        ],
        compiler_params=pltpu.CompilerParams(
            collective_id=0, has_side_effects=True, vmem_limit_bytes=63 * 2**20
        ),
        name="exchange",
    )(key, local, rows, dense, table, accum)


def on_device(layer_input, out_grad, mix_weight, lift_weight, linear_weight, row_ids, row_home, table, row_accum):
    key, local = index_call(row_ids, row_home.reshape(1024, 128))
    rows, dense = layer_call(layer_input, out_grad, mix_weight, lift_weight, linear_weight)
    new_table, new_accum, mix_grad, lift_grad, linear_grad = exchange_call(
        key, local.reshape(8, 8, 128), rows, dense.reshape(2, 512, 128), table, row_accum.reshape(16, 128)
    )
    return (new_table, new_accum.reshape(-1), mix_grad, lift_grad, linear_grad)


def solution(mesh):
    placed = (
        P(("outer", "inner"), None, None),
        P(("outer", "inner"), None, None),
        P(), P(), P(),
        P(("outer", "inner"), None),
        P(),
        P("inner", None),
        P("inner"),
    )
    return jax.shard_map(
        on_device,
        mesh=mesh,
        in_specs=placed,
        out_specs=(P("inner", None), P("inner"), P(), P(), P()),
        check_vma=False,
    )
```

```python
import math

import jax
import jax.numpy as jnp
from jax import lax
from jax.experimental import pallas as pl
from jax.experimental.pallas import tpu as pltpu
from jax.sharding import PartitionSpec as P

LEARN_RATE = 0.5
MESH = pl.DeviceIdType.MESH
BF = jnp.bfloat16
F32 = jnp.float32
VM = pl.BlockSpec(memory_space=pltpu.VMEM)

SAMPLES, FEATS, WIDTH, RANK = 32, 256, 192, 128
BATCH = 8192
HALF = 4096
PIECE = 512
TOGETHER = 4


def dot(a, b, dims=((1,), (0,))):
    return lax.dot_general(a, b, (dims, ((), ())), preferred_element_type=F32)


NT = ((1,), (1,))


def iota(shape, axis):
    return lax.broadcasted_iota(jnp.int32, shape, axis)


def one_hot(rows, row, base):
    near = (row - base).astype(F32).astype(BF)
    tiles = []
    for t in range(row.shape[1] // 128):
        part = jnp.broadcast_to(near[:, t * 128 : (t + 1) * 128], (256, 128))
        tiles.append(jnp.where(rows == part, jnp.ones((), BF), jnp.zeros((), BF)))
    return jnp.concatenate(tiles, axis=1)


def index_kernel(ids_ref, home_ref, key_ref, local_ref, table_t, place_ref):
    home = home_ref[...]
    high = (home >> 9).astype(F32)
    low = ((home & 511) - 256).astype(F32)
    table_t[0:128, :] = high.T.astype(BF)
    table_t[128:256, :] = low.T.astype(BF)
    rows256 = iota((256, 128), 0).astype(F32).astype(BF)
    rows128 = iota((128, 256), 0)

    def look(b, carry):
        ids = ids_ref[pl.ds(b, 1), :]
        high_id = ids >> 7
        hot = jnp.concatenate([one_hot(rows256, high_id, base) for base in (0, 256, 512, 768)], axis=0)
        found = dot(table_t[...], hot)
        mask = rows128 == (ids & 127)
        high_part = jnp.sum(jnp.where(mask, found[0:128], 0.0), axis=0, keepdims=True)
        low_part = jnp.sum(jnp.where(mask, found[128:256], 0.0), axis=0, keepdims=True)
        place_ref[pl.ds(b, 1), :] = (high_part * 512.0 + low_part + 256.0).astype(jnp.int32)
        return carry

    lax.fori_loop(0, SAMPLES, look, 0, unroll=4)
    upper = (iota((256, 256), 0) < iota((256, 256), 1)).astype(F32).astype(BF)
    rows64 = iota((64, 256), 0)
    for half in range(2):

        def rank(step, carry):
            counts, firsts = carry
            b = half * 16 + step
            place = place_ref[pl.ds(b, 1), :]
            owner = place >> 11
            local = place & 2047
            own = (rows64 == owner).astype(F32)
            before = dot(own.astype(BF), upper) + counts
            rank_of = jnp.sum(own * before, axis=0, keepdims=True).astype(jnp.int32)
            key_ref[pl.ds(b, 1), :] = (owner & 7) * 512 + (owner >> 3) * 64 + rank_of
            hot = (rows64 == rank_of).astype(F32).astype(BF)
            parts = jnp.concatenate(
                [own * (local >> 4).astype(F32), own * (local & 15).astype(F32)], axis=0
            ).astype(BF)
            firsts = firsts + dot(parts, hot, NT)
            counts = counts + jnp.sum(own, axis=1, keepdims=True)
            return counts, firsts

        start = (jnp.zeros((64, 1), F32), jnp.zeros((128, 64), F32))
        unused, firsts = lax.fori_loop(0, 16, rank, start, unroll=16)
        merged = firsts[0:64] * 16.0 + firsts[64:128]
        local_ref[:, half * 64 : (half + 1) * 64] = merged.astype(jnp.int32)


def index_call(row_ids, home):
    return pl.pallas_call(
        index_kernel,
        out_shape=(
            jax.ShapeDtypeStruct((SAMPLES, FEATS), jnp.int32),
            jax.ShapeDtypeStruct((64, 128), jnp.int32),
        ),
        in_specs=[VM, VM],
        out_specs=(VM, VM),
        scratch_shapes=[pltpu.VMEM((256, 1024), BF), pltpu.VMEM((SAMPLES, FEATS), jnp.int32)],
        compiler_params=pltpu.CompilerParams(vmem_limit_bytes=63 * 2**20),
        name="index",
    )(row_ids, home)


def layer_kernel(xt_ref, gt_ref, mix_ref, lift_t_ref, linear_ref, rows_ref, dense_ref, left_ref, linear_mix_ref, lift_ref):
    scaling = 1.0 / math.sqrt(WIDTH)

    @pl.when(pl.program_id(0) == 0)
    def _():
        dense_ref[...] = jnp.zeros_like(dense_ref)
        left_ref[...] = mix_ref[...].astype(F32).T.astype(BF)
        lift_ref[...] = lift_t_ref[...].astype(F32).T.astype(BF)
        linear_mix_ref[:, 0:256] = linear_ref[...].astype(F32).T.astype(BF)
        linear_mix_ref[:, 256:384] = mix_ref[...]

    for n in range(TOGETHER):
        xt = xt_ref[n]
        gt = gt_ref[n]
        g = gt.T
        d_products_t = dot(lift_ref[...], gt).astype(BF)
        both = dot(jnp.concatenate([left_ref[...], d_products_t], axis=0), xt, NT)
        compressed_t = both[0:128].astype(BF)
        d_compressed_t = (both[128:256] * scaling).astype(BF)
        next_both = dot(jnp.concatenate([compressed_t, d_compressed_t], axis=0), xt)
        products_t = (next_both[0:128] * scaling).astype(BF)
        d_inputs = g.astype(F32) + dot(
            linear_mix_ref[...], jnp.concatenate([g, d_compressed_t], axis=0)
        )
        d_inputs = d_inputs + scaling * dot(d_products_t.T, compressed_t)
        rows_ref[n * FEATS : (n + 1) * FEATS, :] = d_inputs.astype(BF)
        dense_ref[0:128] += next_both[128:256, 0:128]
        dense_ref[128:256] += next_both[128:256, 128:256]
        linear = dot(g, xt)
        dense_ref[256:512] += linear[:, 0:128]
        dense_ref[512:768] += linear[:, 128:256]
        dense_ref[768:960] += dot(gt, products_t, NT)


def layer_call(xt, gt, mix, lift_t, linear):
    whole = lambda shape: pl.BlockSpec(shape, lambda b: (0, 0))
    return pl.pallas_call(
        layer_kernel,
        grid=(SAMPLES // TOGETHER,),
        out_shape=(
            jax.ShapeDtypeStruct((SAMPLES * FEATS, WIDTH), BF),
            jax.ShapeDtypeStruct((1024, 128), F32),
        ),
        in_specs=[
            pl.BlockSpec((TOGETHER, WIDTH, FEATS), lambda b: (b, 0, 0)),
            pl.BlockSpec((TOGETHER, WIDTH, FEATS), lambda b: (b, 0, 0)),
            whole((256, 128)),
            whole((192, 128)),
            whole((256, 256)),
        ],
        out_specs=(pl.BlockSpec((TOGETHER * FEATS, WIDTH), lambda b: (b, 0)), whole((1024, 128))),
        scratch_shapes=[
            pltpu.VMEM((128, 256), BF), pltpu.VMEM((256, 384), BF), pltpu.VMEM((128, 192), BF),
        ],
        compiler_params=pltpu.CompilerParams(
            vmem_limit_bytes=63 * 2**20, dimension_semantics=("arbitrary",)
        ),
        name="layer",
    )(xt, gt, mix, lift_t, linear)


class Spot:
    def __init__(self):
        outer = lax.axis_index("outer")
        inner = lax.axis_index("inner")
        self.core = lax.rem(outer, 2)
        self.y_lo = outer // 2
        self.x = inner // 16
        self.y_hi = lax.rem(inner // 8, 2)
        self.z = lax.rem(inner, 8)
        self.y = self.y_hi * 2 + self.y_lo

    def at(self, x=None, y=None, z=None, core=None):
        x = self.x if x is None else x
        y = self.y if y is None else y
        z = self.z if z is None else z
        core = self.core if core is None else core
        return (lax.rem(y, 2) * 2 + core, (x * 2 + y // 2) * 8 + z)


def chunk_offset(i):
    return 4 + (1 - 2 * (i % 2)) * ((i + 1) // 2)


def exchange_kernel(
    key_ref, local_ref, rows_any, dense_ref,
    near, far, d_cg,
    rows_ref, send, recv, local_in, own, across, across_in, ring_out, ring_in,
    d_half, d_half_in, d_y_in, d_y, d_x_in, d_z, d_xg, d_yg,
    s_send, s_recv, i_send, i_recv, a_send, a_recv, r_send, r_recv, f_send, f_recv, d_send, d_recv, in_sem,
):
    me = Spot()
    x, y, z, core = me.x, me.y, me.z, me.core
    iota_rows = iota((256, 128), 0).astype(F32).astype(BF)

    def peer(k):
        dx, dy = k // 2, k % 2
        y_to = me.y if dy == 0 else (1 - me.y_hi) * 2 + (1 - me.y_lo)
        return me.at(x=lax.rem(x + dx, 4), y=y_to)

    def place_of(k):
        dx, dy = k // 2, k % 2
        return lax.rem(x + dx, 4) * 2 + (me.y_hi if dy == 0 else 1 - me.y_hi)

    partner = me.at(core=1 - core)
    beside = me.at(y=me.y_hi * 2 + 1 - me.y_lo)
    up = me.at(z=lax.rem(z + 1, 8))
    down = me.at(z=lax.rem(z + 7, 8))
    y_peer = lambda k: me.at(y=lax.rem(y + k, 4))
    x_peer = lambda k: me.at(x=lax.rem(x + k, 4))
    z_peer = lambda k: me.at(z=lax.rem(z + k, 8))

    barrier = pltpu.get_barrier_semaphore()
    greeted = (
        [peer(k) for k in range(1, 8)]
        + [partner]
        + [y_peer(k) for k in (1, 2, 3)]
        + [x_peer(k) for k in (1, 2, 3)]
        + [z_peer(k) for k in range(1, 8)]
    )
    load = pltpu.make_async_copy(rows_any, rows_ref, in_sem)
    load.start()
    for device in greeted:
        pl.semaphore_signal(barrier, inc=1, device_id=device, device_id_type=MESH)
    pl.semaphore_wait(barrier, len(greeted))
    load.wait()

    def copy(src, dst, send_sem, recv_sem, device):
        return pltpu.make_async_remote_copy(
            src_ref=src, dst_ref=dst, send_sem=send_sem, recv_sem=recv_sem,
            device_id=device, device_id_type=MESH,
        )

    def index_copy(k):
        return copy(local_ref.at[place_of(k)], local_in.at[k], i_send.at[k], i_recv.at[k], peer(k))

    def lookup_copy(i, k):
        return copy(send.at[i, place_of(k)], recv.at[i, k], s_send.at[i, k], s_recv.at[i, k], peer(k))

    def across_copy(i):
        return copy(across.at[i], across_in.at[i], a_send.at[i], a_recv.at[i], partner)

    def ring_copy(way, slot):
        return copy(
            ring_out.at[way, slot], ring_in.at[way, slot], r_send.at[way, slot], r_recv.at[way, slot],
            (up, down)[way],
        )

    def chip_copy(p):
        return copy(near.at[core, p], far.at[core, p], f_send.at[0, p], f_recv.at[0, p], beside)

    def core_copy(p):
        return copy(near.at[core, p], near.at[core, p], f_send.at[1, p], f_recv.at[1, p], partner)

    def core_wait(p):
        return copy(near.at[core, p], near.at[1 - core, p], f_send.at[1, p], f_recv.at[1, p], partner)

    def forward_copy(p):
        return copy(far.at[core, p], far.at[core, p], f_send.at[2, p], f_recv.at[2, p], partner)

    def forward_wait(p):
        return copy(far.at[core, p], far.at[1 - core, p], f_send.at[2, p], f_recv.at[2, p], partner)

    def half_copy():
        return copy(dense_ref.at[1 - core], d_half_in, d_send.at[0], d_recv.at[0], partner)

    def y_copy(k):
        return copy(d_half.at[lax.rem(y + k, 4)], d_y_in.at[k - 1], d_send.at[k], d_recv.at[k], y_peer(k))

    def x_copy(k):
        return copy(d_y.at[lax.rem(x + k, 4)], d_x_in.at[k - 1], d_send.at[3 + k], d_recv.at[3 + k], x_peer(k))

    def z_copy(k):
        return copy(d_z.at[z], d_z.at[z], d_send.at[6 + k], d_recv.at[6 + k], z_peer(k))

    def z_wait(k):
        return copy(d_z.at[z], d_z.at[lax.rem(z + 8 - k, 8)], d_send.at[6 + k], d_recv.at[6 + k], z_peer(k))

    def xg_copy(k):
        return copy(d_xg.at[x], d_xg.at[x], d_send.at[13 + k], d_recv.at[13 + k], x_peer(k))

    def xg_wait(k):
        return copy(d_xg.at[x], d_xg.at[lax.rem(x + 4 - k, 4)], d_send.at[13 + k], d_recv.at[13 + k], x_peer(k))

    def yg_copy(k):
        return copy(d_yg.at[y], d_yg.at[y], d_send.at[16 + k], d_recv.at[16 + k], y_peer(k))

    def yg_wait(k):
        return copy(d_yg.at[y], d_yg.at[lax.rem(y + 4 - k, 4)], d_send.at[16 + k], d_recv.at[16 + k], y_peer(k))

    def cg_copy():
        return copy(d_cg.at[core], d_cg.at[core], d_send.at[20], d_recv.at[20], partner)

    def cg_wait():
        return copy(d_cg.at[core], d_cg.at[1 - core], d_send.at[20], d_recv.at[20], partner)

    def dense_1():
        half_copy().start()

    def dense_2():
        half_copy().wait_recv()
        total = dense_ref[core] + d_half_in[...]
        d_half[...] = total.reshape(4, 128, 128)
        for k in (1, 2, 3):
            y_copy(k).start()

    def dense_3():
        for k in (1, 2, 3):
            y_copy(k).wait_recv()
        total = d_half[y] + d_y_in[0] + d_y_in[1] + d_y_in[2]
        d_y[...] = total.reshape(4, 32, 128)
        for k in (1, 2, 3):
            x_copy(k).start()

    def dense_4():
        for k in (1, 2, 3):
            x_copy(k).wait_recv()
        d_z[z] = d_y[x] + d_x_in[0] + d_x_in[1] + d_x_in[2]
        for k in range(1, 8):
            z_copy(k).start()

    def dense_5():
        for k in range(1, 8):
            z_wait(k).wait_recv()
        total = d_z[0]
        for k in range(1, 8):
            total = total + d_z[k]
        d_xg[x] = total * (1.0 / BATCH)
        for k in (1, 2, 3):
            xg_copy(k).start()

    def dense_6():
        for k in (1, 2, 3):
            xg_wait(k).wait_recv()
        d_yg[y] = d_xg[...].reshape(128, 128)
        for k in (1, 2, 3):
            yg_copy(k).start()

    def dense_7():
        for k in (1, 2, 3):
            yg_wait(k).wait_recv()
        d_cg[core] = d_yg[...].reshape(512, 128)
        cg_copy().start()

    def dense_8():
        cg_wait().wait_recv()

    def sort_chunk(i):
        to = lax.rem(z + chunk_offset(i), 8)
        got = []
        for half in range(2):
            total = jnp.zeros((512, WIDTH), F32)
            for t in range(4):
                hot = []
                for part in range(2):
                    base = to * 512 + part * 256
                    tiles = [
                        one_hot(iota_rows, key_ref[pl.ds(half * 16 + t * 4 + b, 1), :], base) for b in range(4)
                    ]
                    hot.append(jnp.concatenate(tiles, axis=1))
                start = half * HALF + t * 1024
                total = total + dot(jnp.concatenate(hot, axis=0), rows_ref[start : start + 1024, :])
            got.append(total)
        for q in range(8):
            at = slice(q * 64, (q + 1) * 64)
            block = jnp.concatenate([got[0][at], got[1][at]], axis=0)
            send[i, q] = block.T.astype(BF)

    def add_chunk(i):
        to = lax.rem(z + chunk_offset(i), 8)
        where = []
        blocks = []
        for k in range(8):
            if k == 0:
                blocks.append(send[i, place_of(0)])
                where.append(local_ref[place_of(0), pl.ds(to, 1), :])
            else:
                lookup_copy(i, k).wait_recv()
                blocks.append(recv[i, k])
                where.append(local_in[k, pl.ds(to, 1), :])
        block = jnp.concatenate(blocks, axis=1)
        row = jnp.concatenate(where, axis=1)
        for mine in (False, True):
            first = (core if mine else 1 - core) * 1024
            for m in range(4):
                total = dot(block, one_hot(iota_rows, row, first + m * 256), NT)
                at = slice(m * 256, (m + 1) * 256)
                if mine:
                    own[i, :, at] = total
                else:
                    across[i, :, at] = total.astype(BF)
            if not mine:
                across_copy(i).start()

    def pieces(i, p):
        at = slice(p * PIECE, (p + 1) * PIECE)
        return own[i, :, at] + across_in[i, :, at].astype(F32)

    for k in range(1, 8):
        index_copy(k).start()
    dense_1()

    def sort_step(i, carry):
        sort_chunk(i)
        for k in range(1, 8):
            lookup_copy(i, k).start()
        return carry

    def add_step(i, carry):
        add_chunk(i)
        return carry

    def ring_send(way, slot, value):
        ring_out[way, slot] = value.astype(BF)
        ring_copy(way, slot).start()

    def ring_got(way, slot):
        ring_copy(way, slot).wait_recv()
        return ring_in[way, slot].astype(F32)

    def ring_level(way, level):
        i = 1 + 2 * level + way
        across_copy(i).wait_recv()
        for slot in (1 + 2 * level, 2 + 2 * level):
            value = pieces(i, (slot + way) % 2)
            if slot >= 2:
                value = value + ring_got(way, slot - 2)
            ring_send(way, slot, value)

    def sorts(first, last):
        lax.fori_loop(first, last, sort_step, 0)

    def adds(first, last):
        lax.fori_loop(first, last, add_step, 0)

    sorts(0, 1)
    dense_2()
    sorts(1, 4)
    for k in range(1, 8):
        index_copy(k).wait_recv()
    adds(0, 1)
    dense_3()
    adds(1, 2)
    across_copy(0).wait_recv()
    ring_send(0, 0, pieces(0, 0))
    ring_send(1, 0, pieces(0, 1))
    sorts(4, 5)
    ring_level(0, 0)
    adds(2, 3)
    sorts(5, 6)
    ring_level(1, 0)
    dense_4()
    adds(3, 4)
    sorts(6, 7)
    ring_level(0, 1)
    adds(4, 5)
    sorts(7, 8)
    ring_level(1, 1)
    dense_5()
    adds(5, 6)
    ring_level(0, 2)
    adds(6, 7)
    ring_level(1, 2)
    dense_6()
    adds(7, 8)
    dense_7()
    across_copy(7).wait_recv()
    for p in (1, 0):
        total = pieces(7, p) + ring_got(0, 6 - p) + ring_got(1, 5 + p)
        near[core, p] = total.astype(BF)
        chip_copy(p).start()
        core_copy(p).start()
    for p in (1, 0):
        chip_copy(p).wait_recv()
        forward_copy(p).start()
    dense_8()
    for p in (1, 0):
        core_wait(p).wait_recv()
        forward_wait(p).wait_recv()

    for k in range(1, 8):
        index_copy(k).wait_send()
        z_copy(k).wait_send()

    def sent(i, carry):
        for k in range(1, 8):
            lookup_copy(i, k).wait_send()
        across_copy(i).wait_send()
        return carry

    lax.fori_loop(0, 8, sent, 0)
    for way in range(2):
        for slot in range(7):
            ring_copy(way, slot).wait_send()
    for p in range(2):
        chip_copy(p).wait_send()
        core_copy(p).wait_send()
        forward_copy(p).wait_send()
    half_copy().wait_send()
    for k in (1, 2, 3):
        y_copy(k).wait_send()
        x_copy(k).wait_send()
        xg_copy(k).wait_send()
        yg_copy(k).wait_send()
    cg_copy().wait_send()


def exchange_call(key, local, rows, dense):
    dma = pltpu.SemaphoreType.DMA
    vmem = pltpu.VMEM
    return pl.pallas_call(
        exchange_kernel,
        out_shape=(
            jax.ShapeDtypeStruct((2, 2, WIDTH, PIECE), BF),
            jax.ShapeDtypeStruct((2, 2, WIDTH, PIECE), BF),
            jax.ShapeDtypeStruct((2, 512, 128), F32),
        ),
        in_specs=[VM, VM, pl.BlockSpec(memory_space=pl.ANY), VM],
        out_specs=(VM,) * 3,
        scratch_shapes=[
            vmem((SAMPLES * FEATS, WIDTH), BF),
            vmem((8, 8, 192, 128), BF),
            vmem((8, 8, 192, 128), BF),
            vmem((8, 8, 128), jnp.int32),
            vmem((8, WIDTH, 1024), F32),
            vmem((8, WIDTH, 1024), BF),
            vmem((8, WIDTH, 1024), BF),
            vmem((2, 7, WIDTH, PIECE), BF),
            vmem((2, 7, WIDTH, PIECE), BF),
            vmem((4, 128, 128), F32),
            vmem((512, 128), F32),
            vmem((3, 128, 128), F32),
            vmem((4, 32, 128), F32),
            vmem((3, 32, 128), F32),
            vmem((8, 32, 128), F32),
            vmem((4, 32, 128), F32),
            vmem((4, 128, 128), F32),
            dma((8, 8)), dma((8, 8)), dma((8,)), dma((8,)), dma((8,)), dma((8,)),
            dma((2, 7)), dma((2, 7)), dma((3, 2)), dma((3, 2)), dma((21,)), dma((21,)), dma(()),
        ],
        compiler_params=pltpu.CompilerParams(
            collective_id=0, has_side_effects=True, vmem_limit_bytes=60 * 2**20
        ),
        name="exchange",
    )(key, local, rows, dense)


def update_kernel(near_ref, far_ref, dense_ref, table_ref, accum_ref, new_table_ref, new_accum_ref, mix_ref, lift_ref, linear_ref):
    step = pl.program_id(0)
    for q in range(4):
        block = slice(q * 128, (q + 1) * 128)
        total = near_ref[0, :, block].astype(F32) + far_ref[0, :, block].astype(F32)
        mean = jnp.sum(total * total, axis=0, keepdims=True) * (1.0 / WIDTH)
        after = accum_ref[pl.ds(step * 4 + q, 1), :] + mean
        new_accum_ref[pl.ds(step * 4 + q, 1), :] = after
        rate = LEARN_RATE / jnp.sqrt(after)
        new_table_ref[:, block] = table_ref[:, block] - total * rate

    @pl.when(step == 0)
    def _():
        mix_ref[0:128, :] = dense_ref[0, 0:128].T
        mix_ref[128:256, :] = dense_ref[0, 128:256].T
        linear_ref[:, 0:128] = dense_ref[0, 256:512]
        linear_ref[:, 128:256] = dense_ref[1, 0:256]
        lift_ref[...] = dense_ref[1, 256:448]


def update_call(near, far, dense, table, accum):
    whole = lambda *shape: pl.BlockSpec(shape, lambda i: (0,) * len(shape))
    columns = pl.BlockSpec((WIDTH, PIECE), lambda i: (0, i))
    return pl.pallas_call(
        update_kernel,
        grid=(4,),
        out_shape=(
            jax.ShapeDtypeStruct((WIDTH, 2048), F32),
            jax.ShapeDtypeStruct((16, 128), F32),
            jax.ShapeDtypeStruct((256, 128), F32),
            jax.ShapeDtypeStruct((192, 128), F32),
            jax.ShapeDtypeStruct((256, 256), F32),
        ),
        in_specs=[
            pl.BlockSpec((1, WIDTH, PIECE), lambda i: (i, 0, 0)),
            pl.BlockSpec((1, WIDTH, PIECE), lambda i: (i, 0, 0)),
            whole(2, 512, 128),
            columns,
            whole(16, 128),
        ],
        out_specs=(columns, whole(16, 128), whole(256, 128), whole(192, 128), whole(256, 256)),
        compiler_params=pltpu.CompilerParams(
            vmem_limit_bytes=63 * 2**20, dimension_semantics=("arbitrary",)
        ),
        name="update",
    )(near.reshape(4, WIDTH, PIECE), far.reshape(4, WIDTH, PIECE), dense, table, accum)


def on_device(layer_input, out_grad, mix_weight, lift_weight, linear_weight, row_ids, row_home, table, row_accum):
    key, local = index_call(row_ids, row_home.reshape(1024, 128))
    rows, dense = layer_call(
        layer_input.transpose(0, 2, 1), out_grad.transpose(0, 2, 1), mix_weight, lift_weight.T, linear_weight
    )
    near, far, dense = exchange_call(key, local.reshape(8, 8, 128), rows, dense.reshape(2, 512, 128))
    new_table, new_accum, mix_grad, lift_grad, linear_grad = update_call(
        near, far, dense, table.T, row_accum.reshape(16, 128)
    )
    return (new_table.T, new_accum.reshape(-1), mix_grad, lift_grad.T, linear_grad)


def solution(mesh):
    placed = (
        P(("outer", "inner"), None, None),
        P(("outer", "inner"), None, None),
        P(), P(), P(),
        P(("outer", "inner"), None),
        P(),
        P("inner", None),
        P("inner"),
    )
    return jax.shard_map(
        on_device,
        mesh=mesh,
        in_specs=placed,
        out_specs=(P("inner", None), P("inner"), P(), P(), P()),
        check_vma=False,
    )
```

```python
import math

import jax
import jax.numpy as jnp
from jax import lax
from jax.experimental import pallas as pl
from jax.experimental.pallas import tpu as pltpu
from jax.sharding import PartitionSpec as P

LEARN_RATE = 0.5
MESH = pl.DeviceIdType.MESH
BF = jnp.bfloat16
F32 = jnp.float32
VM = pl.BlockSpec(memory_space=pltpu.VMEM)

SAMPLES, FEATS, WIDTH, RANK = 32, 256, 192, 128
BATCH = 8192
HALF = 4096
PIECE = 512
TOGETHER = 4


def dot(a, b, dims=((1,), (0,))):
    return lax.dot_general(a, b, (dims, ((), ())), preferred_element_type=F32)


NT = ((1,), (1,))


def iota(shape, axis):
    return lax.broadcasted_iota(jnp.int32, shape, axis)


def one_hot(rows, row, base):
    near = (row - base).astype(F32).astype(BF)
    tiles = []
    for t in range(row.shape[1] // 128):
        part = jnp.broadcast_to(near[:, t * 128 : (t + 1) * 128], (256, 128))
        tiles.append(jnp.where(rows == part, jnp.ones((), BF), jnp.zeros((), BF)))
    return jnp.concatenate(tiles, axis=1)


def index_kernel(ids_ref, home_ref, key_ref, local_ref, table_t, place_ref):
    home = home_ref[...]
    high = (home >> 9).astype(F32)
    low = ((home & 511) - 256).astype(F32)
    table_t[0:128, :] = high.T.astype(BF)
    table_t[128:256, :] = low.T.astype(BF)
    rows256 = iota((256, 128), 0).astype(F32).astype(BF)
    rows128 = iota((128, 256), 0)

    def look(b, carry):
        ids = ids_ref[pl.ds(b, 1), :]
        high_id = ids >> 7
        hot = jnp.concatenate([one_hot(rows256, high_id, base) for base in (0, 256, 512, 768)], axis=0)
        found = dot(table_t[...], hot)
        mask = rows128 == (ids & 127)
        high_part = jnp.sum(jnp.where(mask, found[0:128], 0.0), axis=0, keepdims=True)
        low_part = jnp.sum(jnp.where(mask, found[128:256], 0.0), axis=0, keepdims=True)
        place_ref[pl.ds(b, 1), :] = (high_part * 512.0 + low_part + 256.0).astype(jnp.int32)
        return carry

    lax.fori_loop(0, SAMPLES, look, 0, unroll=4)
    upper = (iota((256, 256), 0) < iota((256, 256), 1)).astype(F32).astype(BF)
    rows64 = iota((64, 256), 0)
    for half in range(2):

        def rank(step, carry):
            counts, firsts = carry
            b = half * 16 + step
            place = place_ref[pl.ds(b, 1), :]
            owner = place >> 11
            local = place & 2047
            own = (rows64 == owner).astype(F32)
            before = dot(own.astype(BF), upper) + counts
            rank_of = jnp.sum(own * before, axis=0, keepdims=True).astype(jnp.int32)
            key_ref[pl.ds(b, 1), :] = (owner & 7) * 512 + (owner >> 3) * 64 + rank_of
            hot = (rows64 == rank_of).astype(F32).astype(BF)
            parts = jnp.concatenate(
                [own * (local >> 4).astype(F32), own * (local & 15).astype(F32)], axis=0
            ).astype(BF)
            firsts = firsts + dot(parts, hot, NT)
            counts = counts + jnp.sum(own, axis=1, keepdims=True)
            return counts, firsts

        start = (jnp.zeros((64, 1), F32), jnp.zeros((128, 64), F32))
        unused, firsts = lax.fori_loop(0, 16, rank, start, unroll=16)
        merged = firsts[0:64] * 16.0 + firsts[64:128]
        local_ref[:, half * 64 : (half + 1) * 64] = merged.astype(jnp.int32)


def index_call(row_ids, home):
    return pl.pallas_call(
        index_kernel,
        out_shape=(
            jax.ShapeDtypeStruct((SAMPLES, FEATS), jnp.int32),
            jax.ShapeDtypeStruct((64, 128), jnp.int32),
        ),
        in_specs=[VM, VM],
        out_specs=(VM, VM),
        scratch_shapes=[pltpu.VMEM((256, 1024), BF), pltpu.VMEM((SAMPLES, FEATS), jnp.int32)],
        compiler_params=pltpu.CompilerParams(vmem_limit_bytes=63 * 2**20),
        name="index",
    )(row_ids, home)


def layer_kernel(xt_ref, gt_ref, mix_ref, lift_t_ref, linear_ref, rows_ref, dense_ref, left_ref, linear_mix_ref, lift_ref):
    scaling = 1.0 / math.sqrt(WIDTH)

    @pl.when(pl.program_id(0) == 0)
    def _():
        dense_ref[...] = jnp.zeros_like(dense_ref)
        left_ref[...] = mix_ref[...].astype(F32).T.astype(BF)
        lift_ref[...] = lift_t_ref[...].astype(F32).T.astype(BF)
        linear_mix_ref[:, 0:256] = linear_ref[...].astype(F32).T.astype(BF)
        linear_mix_ref[:, 256:384] = mix_ref[...]

    for n in range(TOGETHER):
        xt = xt_ref[n]
        gt = gt_ref[n]
        g = gt.T
        d_products_t = dot(lift_ref[...], gt).astype(BF)
        both = dot(jnp.concatenate([left_ref[...], d_products_t], axis=0), xt, NT)
        compressed_t = both[0:128].astype(BF)
        d_compressed_t = (both[128:256] * scaling).astype(BF)
        next_both = dot(jnp.concatenate([compressed_t, d_compressed_t], axis=0), xt)
        products_t = (next_both[0:128] * scaling).astype(BF)
        d_inputs = g.astype(F32) + dot(
            linear_mix_ref[...], jnp.concatenate([g, d_compressed_t], axis=0)
        )
        d_inputs = d_inputs + scaling * dot(d_products_t.T, compressed_t)
        rows_ref[n * FEATS : (n + 1) * FEATS, :] = d_inputs.astype(BF)
        dense_ref[0:128] += next_both[128:256, 0:128]
        dense_ref[128:256] += next_both[128:256, 128:256]
        linear = dot(g, xt)
        dense_ref[256:512] += linear[:, 0:128]
        dense_ref[512:768] += linear[:, 128:256]
        dense_ref[768:960] += dot(gt, products_t, NT)


def layer_call(xt, gt, mix, lift_t, linear):
    whole = lambda shape: pl.BlockSpec(shape, lambda b: (0, 0))
    return pl.pallas_call(
        layer_kernel,
        grid=(SAMPLES // TOGETHER,),
        out_shape=(
            jax.ShapeDtypeStruct((SAMPLES * FEATS, WIDTH), BF),
            jax.ShapeDtypeStruct((1024, 128), F32),
        ),
        in_specs=[
            pl.BlockSpec((TOGETHER, WIDTH, FEATS), lambda b: (b, 0, 0)),
            pl.BlockSpec((TOGETHER, WIDTH, FEATS), lambda b: (b, 0, 0)),
            whole((256, 128)),
            whole((192, 128)),
            whole((256, 256)),
        ],
        out_specs=(pl.BlockSpec((TOGETHER * FEATS, WIDTH), lambda b: (b, 0)), whole((1024, 128))),
        scratch_shapes=[
            pltpu.VMEM((128, 256), BF), pltpu.VMEM((256, 384), BF), pltpu.VMEM((128, 192), BF),
        ],
        compiler_params=pltpu.CompilerParams(
            vmem_limit_bytes=63 * 2**20, dimension_semantics=("arbitrary",)
        ),
        name="layer",
    )(xt, gt, mix, lift_t, linear)


class Spot:
    def __init__(self):
        outer = lax.axis_index("outer")
        inner = lax.axis_index("inner")
        self.core = lax.rem(outer, 2)
        self.y_lo = outer // 2
        self.x = inner // 16
        self.y_hi = lax.rem(inner // 8, 2)
        self.z = lax.rem(inner, 8)
        self.y = self.y_hi * 2 + self.y_lo

    def at(self, x=None, y=None, z=None, core=None):
        x = self.x if x is None else x
        y = self.y if y is None else y
        z = self.z if z is None else z
        core = self.core if core is None else core
        return (lax.rem(y, 2) * 2 + core, (x * 2 + y // 2) * 8 + z)


def chunk_offset(i):
    return 4 + (1 - 2 * (i % 2)) * ((i + 1) // 2)


def exchange_kernel(
    key_ref, local_ref, rows_any, dense_ref,
    near, far, d_cg,
    rows_ref, send, recv, local_in, own, across, across_in, ring_out, ring_in,
    d_half, d_half_in, d_y_in, d_y, d_x_in, d_z, d_xg, d_yg,
    s_send, s_recv, i_send, i_recv, a_send, a_recv, r_send, r_recv, f_send, f_recv, d_send, d_recv, in_sem,
):
    me = Spot()
    x, y, z, core = me.x, me.y, me.z, me.core
    iota_rows = iota((256, 128), 0).astype(F32).astype(BF)

    def peer(k):
        dx, dy = k // 2, k % 2
        y_to = me.y if dy == 0 else (1 - me.y_hi) * 2 + (1 - me.y_lo)
        return me.at(x=lax.rem(x + dx, 4), y=y_to)

    def place_of(k):
        dx, dy = k // 2, k % 2
        return lax.rem(x + dx, 4) * 2 + (me.y_hi if dy == 0 else 1 - me.y_hi)

    partner = me.at(core=1 - core)
    beside = me.at(y=me.y_hi * 2 + 1 - me.y_lo)
    up = me.at(z=lax.rem(z + 1, 8))
    down = me.at(z=lax.rem(z + 7, 8))
    y_peer = lambda k: me.at(y=lax.rem(y + k, 4))
    x_peer = lambda k: me.at(x=lax.rem(x + k, 4))
    z_peer = lambda k: me.at(z=lax.rem(z + k, 8))

    barrier = pltpu.get_barrier_semaphore()
    greeted = (
        [peer(k) for k in range(1, 8)]
        + [partner]
        + [y_peer(k) for k in (1, 2, 3)]
        + [x_peer(k) for k in (1, 2, 3)]
        + [z_peer(k) for k in range(1, 8)]
    )
    load = pltpu.make_async_copy(rows_any, rows_ref, in_sem)
    load.start()
    for device in greeted:
        pl.semaphore_signal(barrier, inc=1, device_id=device, device_id_type=MESH)
    pl.semaphore_wait(barrier, len(greeted))
    load.wait()

    def copy(src, dst, send_sem, recv_sem, device):
        return pltpu.make_async_remote_copy(
            src_ref=src, dst_ref=dst, send_sem=send_sem, recv_sem=recv_sem,
            device_id=device, device_id_type=MESH,
        )

    def index_copy(k):
        return copy(local_ref.at[place_of(k)], local_in.at[k], i_send.at[k], i_recv.at[k], peer(k))

    def lookup_copy(i, k):
        return copy(send.at[i, place_of(k)], recv.at[i, k], s_send.at[i, k], s_recv.at[i, k], peer(k))

    def across_copy(i):
        return copy(across.at[i], across_in.at[i], a_send.at[i], a_recv.at[i], partner)

    def ring_copy(way, slot):
        return copy(
            ring_out.at[way, slot], ring_in.at[way, slot], r_send.at[way, slot], r_recv.at[way, slot],
            (up, down)[way],
        )

    def chip_copy(p):
        return copy(near.at[core, p], far.at[core, p], f_send.at[0, p], f_recv.at[0, p], beside)

    def core_copy(p):
        return copy(near.at[core, p], near.at[core, p], f_send.at[1, p], f_recv.at[1, p], partner)

    def core_wait(p):
        return copy(near.at[core, p], near.at[1 - core, p], f_send.at[1, p], f_recv.at[1, p], partner)

    def forward_copy(p):
        return copy(far.at[core, p], far.at[core, p], f_send.at[2, p], f_recv.at[2, p], partner)

    def forward_wait(p):
        return copy(far.at[core, p], far.at[1 - core, p], f_send.at[2, p], f_recv.at[2, p], partner)

    def half_copy():
        return copy(dense_ref.at[1 - core], d_half_in, d_send.at[0], d_recv.at[0], partner)

    def y_copy(k):
        return copy(d_half.at[lax.rem(y + k, 4)], d_y_in.at[k - 1], d_send.at[k], d_recv.at[k], y_peer(k))

    def x_copy(k):
        return copy(d_y.at[lax.rem(x + k, 4)], d_x_in.at[k - 1], d_send.at[3 + k], d_recv.at[3 + k], x_peer(k))

    def z_copy(k):
        return copy(d_z.at[z], d_z.at[z], d_send.at[6 + k], d_recv.at[6 + k], z_peer(k))

    def z_wait(k):
        return copy(d_z.at[z], d_z.at[lax.rem(z + 8 - k, 8)], d_send.at[6 + k], d_recv.at[6 + k], z_peer(k))

    def xg_copy(k):
        return copy(d_xg.at[x], d_xg.at[x], d_send.at[13 + k], d_recv.at[13 + k], x_peer(k))

    def xg_wait(k):
        return copy(d_xg.at[x], d_xg.at[lax.rem(x + 4 - k, 4)], d_send.at[13 + k], d_recv.at[13 + k], x_peer(k))

    def yg_copy(k):
        return copy(d_yg.at[y], d_yg.at[y], d_send.at[16 + k], d_recv.at[16 + k], y_peer(k))

    def yg_wait(k):
        return copy(d_yg.at[y], d_yg.at[lax.rem(y + 4 - k, 4)], d_send.at[16 + k], d_recv.at[16 + k], y_peer(k))

    def cg_copy():
        return copy(d_cg.at[core], d_cg.at[core], d_send.at[20], d_recv.at[20], partner)

    def cg_wait():
        return copy(d_cg.at[core], d_cg.at[1 - core], d_send.at[20], d_recv.at[20], partner)

    def dense_1():
        half_copy().start()

    def dense_2():
        half_copy().wait_recv()
        total = dense_ref[core] + d_half_in[...]
        d_half[...] = total.reshape(4, 128, 128)
        for k in (1, 2, 3):
            y_copy(k).start()

    def dense_3():
        for k in (1, 2, 3):
            y_copy(k).wait_recv()
        total = d_half[y] + d_y_in[0] + d_y_in[1] + d_y_in[2]
        d_y[...] = total.reshape(4, 32, 128)
        for k in (1, 2, 3):
            x_copy(k).start()

    def dense_4():
        for k in (1, 2, 3):
            x_copy(k).wait_recv()
        d_z[z] = d_y[x] + d_x_in[0] + d_x_in[1] + d_x_in[2]
        for k in range(1, 8):
            z_copy(k).start()

    def dense_5():
        for k in range(1, 8):
            z_wait(k).wait_recv()
        total = d_z[0]
        for k in range(1, 8):
            total = total + d_z[k]
        d_xg[x] = total * (1.0 / BATCH)
        for k in (1, 2, 3):
            xg_copy(k).start()

    def dense_6():
        for k in (1, 2, 3):
            xg_wait(k).wait_recv()
        d_yg[y] = d_xg[...].reshape(128, 128)
        for k in (1, 2, 3):
            yg_copy(k).start()

    def dense_7():
        for k in (1, 2, 3):
            yg_wait(k).wait_recv()
        d_cg[core] = d_yg[...].reshape(512, 128)
        cg_copy().start()

    def dense_8():
        cg_wait().wait_recv()

    def sort_chunk(i):
        to = lax.rem(z + chunk_offset(i), 8)
        got = []
        for half in range(2):
            total = jnp.zeros((512, WIDTH), F32)
            for t in range(4):
                hot = []
                for part in range(2):
                    base = to * 512 + part * 256
                    tiles = [
                        one_hot(iota_rows, key_ref[pl.ds(half * 16 + t * 4 + b, 1), :], base) for b in range(4)
                    ]
                    hot.append(jnp.concatenate(tiles, axis=1))
                start = half * HALF + t * 1024
                total = total + dot(jnp.concatenate(hot, axis=0), rows_ref[start : start + 1024, :])
            got.append(total)
        for q in range(8):
            at = slice(q * 64, (q + 1) * 64)
            block = jnp.concatenate([got[0][at], got[1][at]], axis=0)
            send[i, q] = block.T.astype(BF)

    def add_chunk(i):
        to = lax.rem(z + chunk_offset(i), 8)
        where = []
        blocks = []
        for k in range(8):
            if k == 0:
                blocks.append(send[i, place_of(0)])
                where.append(local_ref[place_of(0), pl.ds(to, 1), :])
            else:
                lookup_copy(i, k).wait_recv()
                blocks.append(recv[i, k])
                where.append(local_in[k, pl.ds(to, 1), :])
        block = jnp.concatenate(blocks, axis=1)
        row = jnp.concatenate(where, axis=1)
        for mine in (False, True):
            first = (core if mine else 1 - core) * 1024
            for m in range(4):
                total = dot(block, one_hot(iota_rows, row, first + m * 256), NT)
                at = slice(m * 256, (m + 1) * 256)
                if mine:
                    own[i, :, at] = total
                else:
                    across[i, :, at] = total.astype(BF)
            if not mine:
                across_copy(i).start()

    def pieces(i, p):
        at = slice(p * PIECE, (p + 1) * PIECE)
        return own[i, :, at] + across_in[i, :, at].astype(F32)

    for k in range(1, 8):
        index_copy(k).start()
    dense_1()

    def sort_step(i, carry):
        sort_chunk(i)
        for k in (2, 6, 1, 4, 3, 7, 5):
            lookup_copy(i, k).start()
        return carry

    def add_step(i, carry):
        add_chunk(i)
        return carry

    def ring_send(way, slot, value):
        ring_out[way, slot] = value.astype(BF)
        ring_copy(way, slot).start()

    def ring_got(way, slot):
        ring_copy(way, slot).wait_recv()
        return ring_in[way, slot].astype(F32)

    def ring_level(way, level):
        i = 1 + 2 * level + way
        across_copy(i).wait_recv()
        for slot in (1 + 2 * level, 2 + 2 * level):
            swapped = way == 1 and level < 2
            value = pieces(i, 1 - slot % 2 if swapped else slot % 2)
            if slot >= 2:
                before = 9 - slot if way == 1 and level == 2 else slot - 2
                value = value + ring_got(way, before)
            ring_send(way, slot, value)

    def sorts(first, last):
        lax.fori_loop(first, last, sort_step, 0)

    def adds(first, last):
        lax.fori_loop(first, last, add_step, 0)

    sorts(0, 1)
    dense_2()
    sorts(1, 4)
    dense_3()
    for k in range(1, 8):
        index_copy(k).wait_recv()
    adds(0, 2)
    across_copy(0).wait_recv()
    ring_send(0, 0, pieces(0, 0))
    ring_send(1, 0, pieces(0, 1))
    sorts(4, 5)
    ring_level(0, 0)
    adds(2, 3)
    dense_4()
    sorts(5, 6)
    ring_level(1, 0)
    adds(3, 4)
    sorts(6, 7)
    ring_level(0, 1)
    adds(4, 5)
    dense_5()
    sorts(7, 8)
    ring_level(1, 1)
    adds(5, 6)
    ring_level(0, 2)
    dense_6()
    adds(6, 7)
    ring_level(1, 2)
    adds(7, 8)
    dense_7()
    across_copy(7).wait_recv()
    for p in (1, 0):
        total = pieces(7, p) + ring_got(0, 6 - p) + ring_got(1, 6 - p)
        near[core, p] = total.astype(BF)
        chip_copy(p).start()
        core_copy(p).start()
    for p in (1, 0):
        chip_copy(p).wait_recv()
        forward_copy(p).start()
    dense_8()
    for p in (1, 0):
        core_wait(p).wait_recv()
        forward_wait(p).wait_recv()

    for k in range(1, 8):
        index_copy(k).wait_send()
        z_copy(k).wait_send()

    def sent(i, carry):
        for k in range(1, 8):
            lookup_copy(i, k).wait_send()
        across_copy(i).wait_send()
        return carry

    lax.fori_loop(0, 8, sent, 0)
    for way in range(2):
        for slot in range(7):
            ring_copy(way, slot).wait_send()
    for p in range(2):
        chip_copy(p).wait_send()
        core_copy(p).wait_send()
        forward_copy(p).wait_send()
    half_copy().wait_send()
    for k in (1, 2, 3):
        y_copy(k).wait_send()
        x_copy(k).wait_send()
        xg_copy(k).wait_send()
        yg_copy(k).wait_send()
    cg_copy().wait_send()


def exchange_call(key, local, rows, dense):
    dma = pltpu.SemaphoreType.DMA
    vmem = pltpu.VMEM
    return pl.pallas_call(
        exchange_kernel,
        out_shape=(
            jax.ShapeDtypeStruct((2, 2, WIDTH, PIECE), BF),
            jax.ShapeDtypeStruct((2, 2, WIDTH, PIECE), BF),
            jax.ShapeDtypeStruct((2, 512, 128), F32),
        ),
        in_specs=[VM, VM, pl.BlockSpec(memory_space=pl.ANY), VM],
        out_specs=(VM,) * 3,
        scratch_shapes=[
            vmem((SAMPLES * FEATS, WIDTH), BF),
            vmem((8, 8, 192, 128), BF),
            vmem((8, 8, 192, 128), BF),
            vmem((8, 8, 128), jnp.int32),
            vmem((8, WIDTH, 1024), F32),
            vmem((8, WIDTH, 1024), BF),
            vmem((8, WIDTH, 1024), BF),
            vmem((2, 7, WIDTH, PIECE), BF),
            vmem((2, 7, WIDTH, PIECE), BF),
            vmem((4, 128, 128), F32),
            vmem((512, 128), F32),
            vmem((3, 128, 128), F32),
            vmem((4, 32, 128), F32),
            vmem((3, 32, 128), F32),
            vmem((8, 32, 128), F32),
            vmem((4, 32, 128), F32),
            vmem((4, 128, 128), F32),
            dma((8, 8)), dma((8, 8)), dma((8,)), dma((8,)), dma((8,)), dma((8,)),
            dma((2, 7)), dma((2, 7)), dma((3, 2)), dma((3, 2)), dma((21,)), dma((21,)), dma(()),
        ],
        compiler_params=pltpu.CompilerParams(
            collective_id=0, has_side_effects=True, vmem_limit_bytes=60 * 2**20
        ),
        name="exchange",
    )(key, local, rows, dense)


def update_kernel(near_ref, far_ref, dense_ref, table_ref, accum_ref, new_table_ref, new_accum_ref, mix_ref, lift_ref, linear_ref):
    step = pl.program_id(0)
    for q in range(8):
        block = slice(q * 128, (q + 1) * 128)
        part = slice(q % 4 * 128, (q % 4 + 1) * 128)
        total = near_ref[q // 4, :, part].astype(F32) + far_ref[q // 4, :, part].astype(F32)
        mean = jnp.sum(total * total, axis=0, keepdims=True) * (1.0 / WIDTH)
        after = accum_ref[pl.ds(step * 8 + q, 1), :] + mean
        new_accum_ref[pl.ds(step * 8 + q, 1), :] = after
        rate = LEARN_RATE / jnp.sqrt(after)
        new_table_ref[:, block] = table_ref[:, block] - total * rate

    @pl.when(step == 0)
    def _():
        mix_ref[0:128, :] = dense_ref[0, 0:128].T
        mix_ref[128:256, :] = dense_ref[0, 128:256].T
        linear_ref[:, 0:128] = dense_ref[0, 256:512]
        linear_ref[:, 128:256] = dense_ref[1, 0:256]
        lift_ref[...] = dense_ref[1, 256:448]


def update_call(near, far, dense, table, accum):
    whole = lambda *shape: pl.BlockSpec(shape, lambda i: (0,) * len(shape))
    columns = pl.BlockSpec((WIDTH, 2 * PIECE), lambda i: (0, i))
    return pl.pallas_call(
        update_kernel,
        grid=(2,),
        out_shape=(
            jax.ShapeDtypeStruct((WIDTH, 2048), F32),
            jax.ShapeDtypeStruct((16, 128), F32),
            jax.ShapeDtypeStruct((256, 128), F32),
            jax.ShapeDtypeStruct((192, 128), F32),
            jax.ShapeDtypeStruct((256, 256), F32),
        ),
        in_specs=[
            pl.BlockSpec((2, WIDTH, PIECE), lambda i: (i, 0, 0)),
            pl.BlockSpec((2, WIDTH, PIECE), lambda i: (i, 0, 0)),
            whole(2, 512, 128),
            columns,
            whole(16, 128),
        ],
        out_specs=(columns, whole(16, 128), whole(256, 128), whole(192, 128), whole(256, 256)),
        compiler_params=pltpu.CompilerParams(
            vmem_limit_bytes=63 * 2**20, dimension_semantics=("arbitrary",)
        ),
        name="update",
    )(near.reshape(4, WIDTH, PIECE), far.reshape(4, WIDTH, PIECE), dense, table, accum)


def on_device(layer_input, out_grad, mix_weight, lift_weight, linear_weight, row_ids, row_home, table, row_accum):
    key, local = index_call(row_ids, row_home.reshape(1024, 128))
    rows, dense = layer_call(
        layer_input.transpose(0, 2, 1), out_grad.transpose(0, 2, 1), mix_weight, lift_weight.T, linear_weight
    )
    near, far, dense = exchange_call(key, local.reshape(8, 8, 128), rows, dense.reshape(2, 512, 128))
    new_table, new_accum, mix_grad, lift_grad, linear_grad = update_call(
        near, far, dense, table.T, row_accum.reshape(16, 128)
    )
    return (new_table.T, new_accum.reshape(-1), mix_grad, lift_grad.T, linear_grad)


def solution(mesh):
    placed = (
        P(("outer", "inner"), None, None),
        P(("outer", "inner"), None, None),
        P(), P(), P(),
        P(("outer", "inner"), None),
        P(),
        P("inner", None),
        P("inner"),
    )
    return jax.shard_map(
        on_device,
        mesh=mesh,
        in_specs=placed,
        out_specs=(P("inner", None), P("inner"), P(), P(), P()),
        check_vma=False,
    )
```
